128 devices in a mesh: fsdp: 8 (over x, z_hi), tensor: 16 (over z_lo, y, core).
Axes of the slice: x: 4, y: 4, z: 4 (z_hi: 2, z_lo: 2; z = z_hi * 2 + z_lo), core: 2. Of those that a mesh axis runs over, the one named last changes fastest.
Arguments:
- tokens: bfloat16 [3072, 8192], P(('fsdp', 'tensor')), may hold values from -6 to 6
- out_grad: bfloat16 [3072, 8192], P(('fsdp', 'tensor')), may hold values from -6 to 6
- up_weight: bfloat16 [256, 8, 128, 128], P('tensor', 'fsdp'), may hold values from -0.1875 to 0.1875
- down_weight: bfloat16 [256, 8, 128, 128], P('tensor', 'fsdp'), may hold values from -0.09375 to 0.09375
- up_index: int32 [256, 8], P('tensor'), may hold values from 0 to 63, all different within a row
- down_index: int32 [256, 8], P('tensor'), may hold values from 0 to 63, all different within a row
Outputs:
- mixed: bfloat16 [3072, 8192], P(('fsdp', 'tensor'))
- input_grad: bfloat16 [3072, 8192], P(('fsdp', 'tensor'))
- up_grad: float32 [256, 8, 128, 128], P('tensor', 'fsdp')
- down_grad: float32 [256, 8, 128, 128], P('tensor', 'fsdp')
The draws below stay inside these ranges and needn't reach their ends.
Inputs may be any that keep to these rules, and one draw needn't show every extreme that they name: Each row of up_index names 8 different input blocks; every block is named somewhere. Each row of down_index names 8 different output blocks; every block is named somewhere.
All inputs are finite; a program needn't handle non-finite values.
Results may differ from the reference program's by a relative error of at most 0.024.
Values may be sent and summed in bfloat16 or wider, within the bound.
A program may use at most 192 MiB of HBM per device.

```python
import jax
import jax.numpy as jnp
from jax import lax

D = 8192
BLK = 128
K = 8
DB = 64
HB = 256
ROWS = 384
TOKENS = 3072
N_FSDP = 8
N_TENSOR = 16


def level_of(key, dims, shards, least, high):
    factor_of = 1.0
    for position, parts in shards:
        steps = jax.random.uniform(jax.random.fold_in(jax.random.fold_in(key, 6), position), (parts,), jnp.float32, least / len(shards), high / len(shards))
        factor_of = factor_of * jnp.repeat(jnp.exp(steps), dims[position] // parts).reshape((-1,) + (1,) * (len(dims) - 1 - position))
    return factor_of


def different_ones(stream_key, rows, count, top, lift):
    order = jax.random.permutation(jax.random.fold_in(stream_key, 1), count)
    favour = order
    for power in range(3):
        favour = favour * favour // count
    favour = favour * lift // count
    chance = jax.random.randint(jax.random.fold_in(stream_key, 2), (rows, count), 0, 4096) + favour
    sure = jax.random.permutation(jax.random.fold_in(stream_key, 3), rows)[jnp.arange(count) % rows]
    chance = jnp.where(jnp.arange(rows)[:, None] == sure[None, :], 1 << 14, chance)
    priority = chance * count + jnp.arange(count)
    return lax.top_k(priority.astype(jnp.int32), top)[1].astype(jnp.int32)


def normal_values(stream_key, extent, scale, limit, shards=(), kind=jnp.bfloat16):
    values = scale * jax.random.normal(stream_key, extent, jnp.float32)
    if shards:
        values = values * level_of(stream_key, extent, shards, -0.22, 0.18)
    return jnp.clip(values, -limit, limit).astype(kind)


def setup_inputs(seed: int = 0) -> dict:
    arg_keys = jax.random.split(jax.random.key(seed), 7)
    return {
        "tokens": normal_values(arg_keys[0], (TOKENS, D), 1.0, 6.0, ((0, 128),)),
        "out_grad": normal_values(arg_keys[1], (TOKENS, D), 1.0, 6.0, ((0, 128),)),
        "up_weight": normal_values(arg_keys[2], (HB, K, BLK, BLK), (K * BLK) ** -0.5, 0.1875, ((0, 16), (1, 8))),
        "down_weight": normal_values(arg_keys[3], (HB, K, BLK, BLK), (HB * K * BLK // DB) ** -0.5, 0.09375, ((0, 16), (1, 8))),
        "up_index": different_ones(arg_keys[4], HB, DB, K, 0),
        "down_index": different_ones(arg_keys[5], HB, DB, K, 0),
    }


def reference(tokens, out_grad, up_weight, down_weight, up_index, down_index):
    input_blocks = tokens.reshape(TOKENS, DB, BLK)
    grad_blocks = out_grad.reshape(TOKENS, DB, BLK)
    per_group = HB // N_TENSOR

    def group_round(slot_terms):
        rounded = lax.optimization_barrier(slot_terms.astype(jnp.bfloat16))
        return jnp.sum(rounded.astype(jnp.float32), axis=0)

    def block_step(carried, scan_items):
        mixed_part, input_part = carried
        up_tile, down_tile, up_row, down_row = scan_items
        chosen = jnp.take(input_blocks, up_row, axis=1)
        preact = jnp.einsum('tki,kio->to', chosen.astype(jnp.float32), up_tile.astype(jnp.float32))
        hidden = jax.nn.silu(preact).astype(jnp.bfloat16)
        outward = jnp.einsum('to,koj->tkj', hidden.astype(jnp.float32), down_tile.astype(jnp.float32))
        mixed_part = mixed_part.at[:, down_row].add(outward)
        picked = jnp.take(grad_blocks, down_row, axis=1)
        hidden_grad = jnp.einsum('tkj,koj->to', picked.astype(jnp.float32), down_tile.astype(jnp.float32))
        gate_sigma = jax.nn.sigmoid(preact)
        pre_grad = (hidden_grad * gate_sigma * (1.0 + preact * (1.0 - gate_sigma))).astype(jnp.bfloat16)
        backward = jnp.einsum('to,kio->tki', pre_grad.astype(jnp.float32), up_tile.astype(jnp.float32))
        input_part = input_part.at[:, up_row].add(backward)
        chosen_g = chosen.astype(jnp.float32).reshape(N_FSDP, ROWS, K, BLK)
        pre_g = pre_grad.astype(jnp.float32).reshape(N_FSDP, ROWS, BLK)
        hidden_g = hidden.astype(jnp.float32).reshape(N_FSDP, ROWS, BLK)
        picked_g = picked.astype(jnp.float32).reshape(N_FSDP, ROWS, K, BLK)
        up_terms = group_round(jnp.einsum('grki,gro->gkio', chosen_g, pre_g))
        down_terms = group_round(jnp.einsum('gro,grkj->gkoj', hidden_g, picked_g))
        return (mixed_part, input_part), (up_terms, down_terms)

    def group_step(totals, group_items):
        empty = (jnp.zeros((TOKENS, DB, BLK), jnp.float32), jnp.zeros((TOKENS, DB, BLK), jnp.float32))
        (mixed_part, input_part), grads = lax.scan(block_step, empty, group_items)
        mixed_total = totals[0] + lax.optimization_barrier(mixed_part.astype(jnp.bfloat16)).astype(jnp.float32)
        input_total = totals[1] + lax.optimization_barrier(input_part.astype(jnp.bfloat16)).astype(jnp.float32)
        return (mixed_total, input_total), grads

    group_items = (up_weight.reshape(N_TENSOR, per_group, K, BLK, BLK),
                   down_weight.reshape(N_TENSOR, per_group, K, BLK, BLK),
                   up_index.reshape(N_TENSOR, per_group, K),
                   down_index.reshape(N_TENSOR, per_group, K))
    begin = (jnp.zeros((TOKENS, DB, BLK), jnp.float32), jnp.zeros((TOKENS, DB, BLK), jnp.float32))
    (mixed_total, input_total), (up_grad, down_grad) = lax.scan(group_step, begin, group_items)
    mixed = mixed_total.reshape(TOKENS, D).astype(jnp.bfloat16)
    input_grad = input_total.reshape(TOKENS, D).astype(jnp.bfloat16)
    return mixed, input_grad, up_grad.reshape(HB, K, BLK, BLK), down_grad.reshape(HB, K, BLK, BLK)
```

```python
import functools

import jax
import jax.numpy as jnp
from jax import lax
from jax.experimental import pallas as pl
from jax.experimental.pallas import tpu as pltpu
from jax.sharding import PartitionSpec as P

MESH = pl.DeviceIdType.MESH
F32, BF = jnp.float32, jnp.bfloat16
BLK = 128


def place():
    f = lax.axis_index("fsdp"); t = lax.axis_index("tensor")
    return f // 2, f % 2, (t // 2) % 4, t // 8, t % 2

def fdev(x, zh): return x * 2 + zh
def tdev(y, zl, c): return (zl * 4 + y) * 2 + c

def gather_kernel(do_f, do_t, do_e, tok, og, upw, dww, tok_o, og_o, up_o, dw_o, ss, rs, ls):
    x, zh, y, zl, c = place()
    f, t = fdev(x, zh), tdev(y, zl, c)
    xp, xm = (x + 1) % 4, (x + 3) % 4
    yp, ym = (y + 1) % 4, (y + 3) % 4
    FP, FM, FZ = (fdev(xp, zh), t), (fdev(xm, zh), t), (fdev(x, 1 - zh), t)
    TP, TM, TZ, TC = (f, tdev(yp, zl, c)), (f, tdev(ym, zl, c)), (f, tdev(y, 1 - zl, c)), (f, tdev(y, zl, 1 - c))
    barrier = pltpu.get_barrier_semaphore()
    for d in (FP, FM, FZ, TP, TM, TZ, TC):
        pl.semaphore_signal(barrier, inc=1, device_id=d, device_id_type=MESH)
    pl.semaphore_wait(barrier, 7)
    n = [0]
    allc = []
    def send(src, dst, dev):
        i = n[0]; n[0] += 1
        cp = pltpu.make_async_remote_copy(src_ref=src, dst_ref=dst, send_sem=ss.at[i], recv_sem=rs.at[i], device_id=dev, device_id_type=MESH)
        cp.start(); allc.append(cp); return cp
    local = []
    def view(o, s):
        return o.at[pl.ds(pl.multiple_of(s * 24, 8), 24)] if len(o.shape) == 2 else o.at[s]
    for i, (s, d) in enumerate(((tok, view(tok_o, t)), (og, view(og_o, t)), (upw, up_o.at[f]), (dww, dw_o.at[f]))):
        cp = pltpu.make_async_copy(s, d, ls.at[i]); cp.start(); local.append(cp)
    got = set()
    def arrive(cp):
        if id(cp) not in got:
            got.add(id(cp)); cp.wait_recv()
    def view(o, s):
        return o.at[pl.ds(pl.multiple_of(s * 24, 8), 24)] if len(o.shape) == 2 else o.at[s]
    W = ((upw, up_o), (dww, dw_o)); A = ((tok, tok_o), (og, og_o))
    fs = lambda x_, z_: fdev(x_, z_)
    ts = lambda y_, z_: tdev(y_, z_, c)
    def first(net, slot, a, z, Pd, Md, Zd):
        h = {}
        for m in (0, 1): h["p", m] = send(net[m][0], view(net[m][1], slot(a, z)), Pd)
        for m in (1, 0): h["m", m] = send(net[m][0], view(net[m][1], slot(a, z)), Md)
        for m in (0, 1): h["z", m] = send(net[m][0], view(net[m][1], slot(a, z)), Zd)
        return h
    def relay_own(h, net, slot, a, ap, am, z, Pd, Md):
        arrive(h["p", 0]); s = slot(am, z); h["dp"] = send(view(net[0][1], s), view(net[0][1], s), Pd)
        arrive(h["m", 1]); s = slot(ap, z); h["dm"] = send(view(net[1][1], s), view(net[1][1], s), Md)
    def cross(h, net, slot, a, z, Pd, Md):
        for m in (0, 1):
            arrive(h["z", m]); s = slot(a, 1 - z)
            h["cp", m] = send(view(net[m][1], s), view(net[m][1], s), Pd)
            h["cm", m] = send(view(net[m][1], s), view(net[m][1], s), Md)
    def relay_oth(h, net, slot, a, ap, am, z, Pd, Md):
        arrive(h["cp", 0]); s = slot(am, 1 - z); h["ep"] = send(view(net[0][1], s), view(net[0][1], s), Pd)
        arrive(h["cm", 1]); s = slot(ap, 1 - z); h["em"] = send(view(net[1][1], s), view(net[1][1], s), Md)
    e = []
    def share(m, s):
        if do_e: e.append(send(view(A[m][1], s), view(A[m][1], s), TC))
    if do_t: ht = first(A, ts, y, zl, TP, TM, TZ)
    if do_f: hf = first(W, fs, x, zh, FP, FM, FZ)
    if do_e:
        for m in (0, 1): e.append(send(A[m][0], view(A[m][1], t), TC))
    if do_t:
        relay_own(ht, A, ts, y, yp, ym, zl, TP, TM)
    if do_f: relay_own(hf, W, fs, x, xp, xm, zh, FP, FM)
    if do_t:
        cross(ht, A, ts, y, zl, TP, TM)
    if do_f: cross(hf, W, fs, x, zh, FP, FM)
    if do_t:
        share(0, ts(ym, zl)); share(1, ts(yp, zl)); share(0, ts(y, 1 - zl)); share(1, ts(y, 1 - zl))
        arrive(ht["p", 1]); share(1, ts(ym, zl)); arrive(ht["m", 0]); share(0, ts(yp, zl))
        relay_oth(ht, A, ts, y, yp, ym, zl, TP, TM)
        share(0, ts(ym, 1 - zl)); share(1, ts(yp, 1 - zl))
    if do_f: relay_oth(hf, W, fs, x, xp, xm, zh, FP, FM)
    if do_t:
        y2 = (y + 2) % 4
        arrive(ht["dp"]); share(0, ts(y2, zl)); arrive(ht["dm"]); share(1, ts(y2, zl))
        arrive(ht["cp", 1]); share(1, ts(ym, 1 - zl)); arrive(ht["cm", 0]); share(0, ts(yp, 1 - zl))
        arrive(ht["ep"]); share(0, ts(y2, 1 - zl)); arrive(ht["em"]); share(1, ts(y2, 1 - zl))
    for cp in allc: arrive(cp)
    for cp in allc: cp.wait_send()
    for cp in local: cp.wait()

def gather_all(tok, og, upw, dww, do_f=True, do_t=True, do_e=True, cid=0):
    bf = jnp.bfloat16
    sh = jax.ShapeDtypeStruct
    return pl.pallas_call(
        functools.partial(gather_kernel, do_f, do_t, do_e),
        out_shape=(sh((384, 8192), bf), sh((384, 8192), bf), sh((8, 16, 128, 128), bf), sh((8, 16, 128, 128), bf)),
        in_specs=[pl.BlockSpec(memory_space=pl.ANY)] * 4,
        out_specs=tuple([pl.BlockSpec(memory_space=pl.ANY)] * 4),
        scratch_shapes=[pltpu.SemaphoreType.DMA((48,)), pltpu.SemaphoreType.DMA((48,)), pltpu.SemaphoreType.DMA((4,))],
        compiler_params=pltpu.CompilerParams(collective_id=cid, has_side_effects=True),
        name="gather_all",
    )(tok, og, upw, dww)


def block_of(ref, b):
    return ref.at[:, pl.ds(pl.multiple_of(b * BLK, BLK), BLK)]

def lanes(tiles):
    return jnp.concatenate([tiles[k, 0] for k in range(8)], axis=1)

def tile_kernel(ui, di, tok, og, wu, wd, mix_o, inp_o, ug_o, dg_o, xs, gs, am, ai):
    j = pl.program_id(0)
    @pl.when(j == 0)
    def _():
        am[...] = jnp.zeros_like(am); ai[...] = jnp.zeros_like(ai)
    for k in range(8):
        xs[:, k * BLK:(k + 1) * BLK] = block_of(tok, ui[j, k])[...]
        gs[:, k * BLK:(k + 1) * BLK] = block_of(og, di[j, k])[...]
    wu2 = wu[...].reshape(1024, BLK)
    wd2 = lanes(wd)
    pre = jnp.dot(xs[...], wu2, preferred_element_type=F32)
    s = 1.0 / (1.0 + jnp.exp(-pre))
    hidden = (pre * s).astype(BF)
    hg = lax.dot_general(gs[...], wd2, (((1,), (1,)), ((), ())), preferred_element_type=F32)
    pg = (hg * s * (1.0 + pre * (1.0 - s))).astype(BF)
    dg = lax.dot_general(hidden, gs[...], (((0,), (0,)), ((), ())), preferred_element_type=F32)
    ug = lax.dot_general(pg, xs[...], (((0,), (0,)), ((), ())), preferred_element_type=F32)
    for k in range(8):
        dg_o[k, 0] = dg[:, k * BLK:(k + 1) * BLK].astype(BF)
        ug_o[k, 0] = ug[:, k * BLK:(k + 1) * BLK].astype(BF)
    out = jnp.dot(hidden, wd2, preferred_element_type=F32)
    for k in range(8):
        r = block_of(am, di[j, k]); r[...] += out[:, k * BLK:(k + 1) * BLK]
    back = lax.dot_general(pg, wu2, (((1,), (1,)), ((), ())), preferred_element_type=F32)
    for k in range(8):
        r = block_of(ai, ui[j, k]); r[...] += back[:, k * BLK:(k + 1) * BLK]
    @pl.when(j == 15)
    def _():
        mix_o[...] = am[...].astype(BF); inp_o[...] = ai[...].astype(BF)

def tiles(ui, di, tok, og, wu, wd):
    sh = jax.ShapeDtypeStruct
    one = pl.Buffered(1)
    whole = pl.BlockSpec((384, 8192), lambda j, *_: (0, 0), pipeline_mode=one)
    part = pl.BlockSpec((8, 1, BLK, BLK), lambda j, *_: (0, j, 0, 0))
    return pl.pallas_call(
        tile_kernel,
        out_shape=(sh((384, 8192), BF), sh((384, 8192), BF), sh((8, 16, BLK, BLK), BF), sh((8, 16, BLK, BLK), BF)),
        grid_spec=pltpu.PrefetchScalarGridSpec(
            num_scalar_prefetch=2, grid=(16,),
            in_specs=[whole, whole, part, part],
            out_specs=(whole, whole, part, part),
            scratch_shapes=[pltpu.VMEM((384, 1024), BF), pltpu.VMEM((384, 1024), BF), pltpu.VMEM((384, 8192), F32), pltpu.VMEM((384, 8192), F32)]),
        compiler_params=pltpu.CompilerParams(vmem_limit_bytes=62 << 20),
        cost_estimate=pl.CostEstimate(flops=10_000_000_000, bytes_accessed=42_000_000, transcendentals=800_000),
        name="tiles",
    )(ui, di, tok, og, wu, wd)


def scatter_kernel(mix, inp, upg, dng, mix_o, inp_o, up_o, dn_o,
                   pf, rf, zf, xf, pt, ct, rt, zt, ss, rs, ls):
    x, zh, y, zl, c = place()
    f, t = fdev(x, zh), tdev(y, zl, c)
    xp, xm, x2 = (x + 1) % 4, (x + 3) % 4, (x + 2) % 4
    yp, ym, y2 = (y + 1) % 4, (y + 3) % 4, (y + 2) % 4
    FP, FM, FZ = (fdev(xp, zh), t), (fdev(xm, zh), t), (fdev(x, 1 - zh), t)
    TP, TM, TZ, TC = (f, tdev(yp, zl, c)), (f, tdev(ym, zl, c)), (f, tdev(y, 1 - zl, c)), (f, tdev(y, zl, 1 - c))
    G = (upg, dng)
    A = (mix, inp)
    nl = [0]; local = {}
    def rows(ref, s):
        return ref.at[pl.ds(pl.multiple_of(s * 24, 8), 24)]
    def load(key, src, dst):
        cp = pltpu.make_async_copy(src, dst, ls.at[nl[0]]); nl[0] += 1
        cp.start(); local[key] = cp
    chips = [(yy, zz) for zz in (0, 1) for yy in (2, 1, 3, 0)]
    def chip(rel):
        dy, own = rel
        return (y + dy) % 4, (zl if own else 1 - zl)
    fk = [(dx, own) for own in (0, 1) for dx in (1, 3, 0)]
    for rel in chips:
        for m in (0, 1):
            yy, zz = chip(rel)
            load(("t", m, rel), rows(A[m], tdev(yy, zz, c)), pt.at[m, rel[1] * 4 + rel[0]])
    for m, dx, own in ((0, 1, 0), (1, 3, 0), (0, 1, 1), (1, 3, 1), (0, 0, 0), (1, 0, 0), (0, 0, 1), (1, 0, 1)):
        load(("f", m, dx, own), G[m].at[fdev((x + dx) % 4, zh if own else 1 - zh)], pf.at[m, own * 2 + (1 if dx else 0)])
    barrier = pltpu.get_barrier_semaphore()
    for d in (FP, FM, FZ, TP, TM, TZ, TC):
        pl.semaphore_signal(barrier, inc=1, device_id=d, device_id_type=MESH)
    pl.semaphore_wait(barrier, 7)
    n = [0]; sent = []
    def send(src, dst, dev):
        i = n[0]; n[0] += 1
        cp = pltpu.make_async_remote_copy(src_ref=src, dst_ref=dst, send_sem=ss.at[i], recv_sem=rs.at[i], device_id=dev, device_id_type=MESH)
        cp.start(); sent.append(cp); return cp
    h = {}
    for rel in chips:
        for m in (0, 1):
            yy, zz = chip(rel)
            h["c", m, rel] = send(rows(A[m], tdev(yy, zz, 1 - c)), ct.at[m, rel[1] * 4 + rel[0]], TC)
    for own in (0, 1):
        zz = zh if own else 1 - zh
        h["ru", own] = send(G[0].at[fdev(x2, zz)], rf.at[0, 0, own], FP)
        h["rd", own] = send(G[1].at[fdev(x2, zz)], rf.at[1, 0, own], FM)
    for own in (0, 1):
        zz = zh if own else 1 - zh
        h["du", own] = send(G[0].at[fdev(xm, zz)], rf.at[0, 1, own], FM)
        h["dd", own] = send(G[1].at[fdev(xp, zz)], rf.at[1, 1, own], FP)

    def add_tiles(dst, a, b, e=None):
        @pl.loop(0, 8)
        def _(i):
            q = pl.ds(i * 2, 2)
            v = a[q].astype(F32) + b[q].astype(F32)
            if e is not None: v = v + e[q].astype(F32)
            dst[q] = v.astype(dst.dtype)
    def add_rows(dst, a, b, e=None):
        @pl.loop(0, 8)
        def _(i):
            q = pl.ds(pl.multiple_of(i * 1024, 1024), 1024)
            v = a[:, q].astype(F32) + b[:, q].astype(F32)
            if e is not None: v = v + e[:, q].astype(F32)
            dst[:, q] = v.astype(dst.dtype)

    def pair(m, rel):
        h["c", m, rel].wait_recv(); local["t", m, rel].wait()
        s = rel[1] * 4 + rel[0]
        add_rows(pt.at[m, s], pt.at[m, s], ct.at[m, s])
    for own in (0, 1):
        pair(0, (2, own)); h["r0", own] = send(pt.at[0, own * 4 + 2], rt.at[0, 0, own], TP)
        pair(1, (2, own)); h["r1", own] = send(pt.at[1, own * 4 + 2], rt.at[1, 0, own], TM)
    for own in (0, 1):
        pair(0, (3, own)); h["d0", own] = send(pt.at[0, own * 4 + 3], rt.at[0, 1, own], TM)
        pair(1, (1, own)); h["d1", own] = send(pt.at[1, own * 4 + 1], rt.at[1, 1, own], TP)
    for own in (0, 1):
        pair(0, (1, own)); pair(1, (3, own))
        h["r0", own].wait_recv(); add_rows(pt.at[0, own * 4 + 1], pt.at[0, own * 4 + 1], rt.at[0, 0, own])
        h["f0", own] = send(pt.at[0, own * 4 + 1], rt.at[0, 2, own], TP)
        h["r1", own].wait_recv(); add_rows(pt.at[1, own * 4 + 3], pt.at[1, own * 4 + 3], rt.at[1, 0, own])
        h["f1", own] = send(pt.at[1, own * 4 + 3], rt.at[1, 2, own], TM)
        local["f", 0, 1, own].wait(); h["ru", own].wait_recv()
        add_tiles(pf.at[0, own * 2 + 1], pf.at[0, own * 2 + 1], rf.at[0, 0, own])
        h["fu", own] = send(pf.at[0, own * 2 + 1], rf.at[0, 2, own], FP)
        local["f", 1, 3, own].wait(); h["rd", own].wait_recv()
        add_tiles(pf.at[1, own * 2 + 1], pf.at[1, own * 2 + 1], rf.at[1, 0, own])
        h["fd", own] = send(pf.at[1, own * 2 + 1], rf.at[1, 2, own], FM)
    for own in (0, 1):
        pair(0, (0, own)); pair(1, (0, own))
        for m in (0, 1):
            h["d%d" % m, own].wait_recv(); h["f%d" % m, own].wait_recv()
            if own == 0:
                add_rows(pt.at[m, 0], pt.at[m, 0], rt.at[m, 1, 0], rt.at[m, 2, 0])
                h["zt", m] = send(pt.at[m, 0], zt.at[m], TZ)
            else:
                h["zt", m].wait_recv()
                add_rows(pt.at[m, 4], pt.at[m, 4], rt.at[m, 1, 1], rt.at[m, 2, 1])
                add_rows((mix_o, inp_o)[m], pt.at[m, 4], zt.at[m])
        for m in (0, 1):
            local["f", m, 0, own].wait()
            h[("du", "dd")[m], own].wait_recv(); h[("fu", "fd")[m], own].wait_recv()
            if own == 0:
                add_tiles(xf.at[m], pf.at[m, 0], rf.at[m, 1, 0], rf.at[m, 2, 0])
                h["zf", m] = send(xf.at[m], zf.at[m], FZ)
            else:
                h["zf", m].wait_recv()
                o = (up_o, dn_o)[m]
                add_tiles(o, pf.at[m, 2], rf.at[m, 1, 1], rf.at[m, 2, 1])
                @pl.loop(0, 8)
                def _(i):
                    q = pl.ds(i * 2, 2)
                    o[q] = o[q] + zf[m, q].astype(F32)
    for cp in sent: cp.wait_send()

def scatter_all(mix, inp, upg, dng, cid=1):
    sh = jax.ShapeDtypeStruct
    V = pltpu.VMEM
    D = 8192
    T = (16, BLK, BLK)
    return pl.pallas_call(
        scatter_kernel,
        out_shape=(sh((24, D), BF), sh((24, D), BF), sh(T, F32), sh(T, F32)),
        in_specs=[pl.BlockSpec(memory_space=pl.ANY)] * 4,
        out_specs=tuple([pl.BlockSpec(memory_space=pltpu.VMEM)] * 4),
        scratch_shapes=[V((2, 4) + T, BF), V((2, 3, 2) + T, BF), V((2,) + T, BF), V((2,) + T, BF),
                        V((2, 8, 24, D), BF), V((2, 8, 24, D), BF), V((2, 3, 2, 24, D), BF), V((2, 24, D), BF),
                        pltpu.SemaphoreType.DMA((48,)), pltpu.SemaphoreType.DMA((48,)), pltpu.SemaphoreType.DMA((32,))],
        compiler_params=pltpu.CompilerParams(collective_id=cid, has_side_effects=True, vmem_limit_bytes=56 << 20),
        name="scatter_all",
    )(mix, inp, upg, dng)


def body(tokens, out_grad, up_weight, down_weight, up_index, down_index):
    T, G, WU, WD = gather_all(tokens, out_grad, up_weight[:, 0], down_weight[:, 0])
    M, I, U, D = tiles(up_index, down_index, T, G, WU, WD)
    mixed, input_grad, up_grad, down_grad = scatter_all(M, I, U, D)
    return mixed, input_grad, up_grad.transpose(0, 2, 1)[:, None], down_grad[:, None]


def solution(mesh):
    rows = P(("fsdp", "tensor"), None)
    tile = P("tensor", "fsdp", None, None)
    index = P("tensor", None)
    return jax.shard_map(
        body,
        mesh=mesh,
        in_specs=(rows, rows, tile, tile, index, index),
        out_specs=(rows, rows, tile, tile),
        check_vma=False,
    )
```

```python
import jax
import jax.numpy as jnp
from jax import lax
from jax.experimental import pallas as pl
from jax.experimental.pallas import tpu as pltpu
from jax.sharding import PartitionSpec as P

MESH = pl.DeviceIdType.MESH
F32, BF = jnp.float32, jnp.bfloat16
BLK = 128
D = 8192
NQ = 4
NB = D // BLK
NH = 2


def place():
    f = lax.axis_index("fsdp")
    t = lax.axis_index("tensor")
    return f // 2, f % 2, (t // 2) % 4, t // 8, t % 2


def fdev(x, zh):
    return x * 2 + zh


def tdev(y, zl, c):
    return (zl * 4 + y) * 2 + c


def step_kernel(tok, og, upw, dnw, ui, di, mix_o, inp_o, up_o, dn_o,
                raw, mine, TK, OG, WU, WD, hid, pgs, xs, gs, GP, rf, zf, pt, ct, rt, zt, tabv, tab, ss, rs, ls):
    x, zh, y, zl, c = place()
    f, t = fdev(x, zh), tdev(y, zl, c)
    xp, xm, x2 = (x + 1) % 4, (x + 3) % 4, (x + 2) % 4
    yp, ym, y2 = (y + 1) % 4, (y + 3) % 4, (y + 2) % 4
    FP, FM, FZ = (fdev(xp, zh), t), (fdev(xm, zh), t), (fdev(x, 1 - zh), t)
    TP, TM, TZ, TC = (f, tdev(yp, zl, c)), (f, tdev(ym, zl, c)), (f, tdev(y, 1 - zl, c)), (f, tdev(y, zl, 1 - c))
    JQ = 16 // NQ
    CH = NB // NH
    count = {"r": 0, "l": 0}
    sends = {"a": [], "w": [], "g": []}
    got = set()

    def send(group, src, dst, dev):
        i = count["r"]
        count["r"] += 1
        cp = pltpu.make_async_remote_copy(src_ref=src, dst_ref=dst, send_sem=ss.at[i], recv_sem=rs.at[i],
                                          device_id=dev, device_id_type=MESH)
        cp.start()
        sends[group].append(cp)
        return cp

    def arrive(cp):
        if id(cp) not in got:
            got.add(id(cp))
            cp.wait_recv()

    def local(src, dst):
        i = count["l"]
        count["l"] += 1
        cp = pltpu.make_async_copy(src, dst, ls.at[i])
        cp.start()
        return cp

    def rows(ref, s, col=None):
        r = pl.ds(pl.multiple_of(s * 24, 8), 24)
        return ref.at[:, r] if col is None else ref.at[pl.ds(col * CH, CH), r]

    raws = [local(tok, raw.at[0]), local(og, raw.at[1])]

    lane = lax.broadcasted_iota(jnp.int32, (16, BLK), 1)
    row = lax.broadcasted_iota(jnp.int32, (16, BLK), 0)
    for m, ref in ((0, di), (1, ui)):
        idx = ref[...]
        table = jnp.full((16, BLK), BLK, jnp.int32)
        for k in range(8):
            col = jnp.broadcast_to(idx[:, k:k + 1], (16, BLK))
            table = jnp.where(col == lane, k * 16 + row, table)
            table = jnp.where(lane == 64 + k, col, table)
        tabv[pl.ds(m * 16, 16), :] = table
    table_copy = local(tabv, tab)
    WU[BLK] = jnp.zeros((BLK, BLK), BF)
    WD[BLK] = jnp.zeros((BLK, BLK), BF)
    own = [local(upw, WU.at[pl.ds(f * 16, 16)]), local(dnw, WD.at[pl.ds(f * 16, 16)])]

    barrier = pltpu.get_barrier_semaphore()
    for d in (FP, FM, FZ, TP, TM, TZ, TC):
        pl.semaphore_signal(barrier, inc=1, device_id=d, device_id_type=MESH)
    pl.semaphore_wait(barrier, 7)

    h = {}

    class Net:
        def __init__(self, group, a, ap, am, z, P_, M_, Z_, mine, at):
            self.g, self.a, self.ap, self.am, self.z, self.P, self.M, self.Z = group, a, ap, am, z, P_, M_, Z_
            self.mine, self.at = mine, at

        def key(self, n, q):
            return self.g + n, q

        def out(self, name, m, q, a, z, dev, first=False):
            dst = self.at(m, a, z, q)
            h[self.g, name, m, q] = send(self.g, self.mine(m, q) if first else dst, dst, dev)

        def s1(self, q):
            for name, m, dev in (("p", 0, self.P), ("m", 1, self.M), ("z", 0, self.Z), ("z", 1, self.Z), ("p", 1, self.P), ("m", 0, self.M)):
                self.out(name, m, q, self.a, self.z, dev, True)

        def come(self, name, m, q):
            arrive(h[self.g, name, m, q])

        def s2(self, q):
            self.come("p", 0, q)
            self.out("d", 0, q, self.am, self.z, self.P)
            self.come("m", 1, q)
            self.out("d", 1, q, self.ap, self.z, self.M)
            for m in (0, 1):
                self.come("z", m, q)
                for name, dev in ((("cp", self.P), ("cm", self.M)), (("cm", self.M), ("cp", self.P)))[m]:
                    self.out(name, m, q, self.a, 1 - self.z, dev)

        def s3(self, q):
            self.come("cp", 0, q)
            self.out("e", 0, q, self.am, 1 - self.z, self.P)
            self.come("cm", 1, q)
            self.out("e", 1, q, self.ap, 1 - self.z, self.M)

        def rest(self, q):
            for name, m in (("p", 1), ("m", 0), ("d", 0), ("d", 1), ("cp", 1), ("cm", 0), ("e", 0), ("e", 1)):
                self.come(name, m, q)

    W = (WU, WD)
    A = (TK, OG)
    wn = Net("w", x, xp, xm, zh, FP, FM, FZ,
             lambda m, q: (upw, dnw)[m].at[pl.ds(q * JQ, JQ)],
             lambda m, a, z, q: W[m].at[pl.ds(fdev(a, z) * 16 + q * JQ, JQ)])
    an = Net("a", y, yp, ym, zl, TP, TM, TZ,
             lambda m, q: mine.at[m, pl.ds(q * CH, CH)],
             lambda m, a, z, q: rows(A[m], tdev(a, z, c), q))
    shares = []

    def share(q, *items):
        for m, a, z in items:
            ref = an.at(m, a, z, q)
            shares.append(send("a", ref, ref, TC))

    wn.s1(0)
    for m in (0, 1):
        raws[m].wait()
        for b in range(NB):
            mine[m, b] = raw[m, :, b * BLK:(b + 1) * BLK]
    an.s1(0)
    own += [local(mine.at[m], rows(A[m], t)) for m in (0, 1)]
    wn.s1(1)
    an.s1(1)
    for q in range(NH):
        for m in (0, 1):
            shares.append(send("a", an.mine(m, q), an.at(m, y, zl, q), TC))
    wn.s2(0)
    an.s2(0)
    share(0, (0, ym, zl), (1, yp, zl), (0, y, 1 - zl), (1, y, 1 - zl))
    wn.s1(2)
    wn.s2(1)
    wn.s3(0)
    an.s2(1)
    share(1, (0, ym, zl), (1, yp, zl), (0, y, 1 - zl), (1, y, 1 - zl))
    wn.s1(3)
    an.s3(0)
    share(0, (0, ym, 1 - zl), (1, yp, 1 - zl))
    wn.s2(2)
    wn.s3(1)
    an.s3(1)
    share(1, (0, ym, 1 - zl), (1, yp, 1 - zl))
    wn.s2(3)
    wn.s3(2)
    for q in range(NH):
        an.rest(q)
        share(q, (1, ym, zl), (0, yp, zl), (0, y2, zl), (1, y2, zl), (1, ym, 1 - zl), (0, yp, 1 - zl), (0, y2, 1 - zl), (1, y2, 1 - zl))
    wn.s3(3)
    wn.rest(0)
    for cp in own:
        cp.wait()
    table_copy.wait()
    for cp in shares:
        arrive(cp)

    def products(q):
        @pl.loop(q * JQ, (q + 1) * JQ)
        def _(j):
            for k in range(8):
                xs[:, k * BLK:(k + 1) * BLK] = TK[tab[16 + j, 64 + k]]
                gs[:, k * BLK:(k + 1) * BLK] = OG[tab[j, 64 + k]]
            wu = jnp.concatenate([WU[k * 16 + j] for k in range(8)], axis=0)
            wd = jnp.concatenate([WD[k * 16 + j] for k in range(8)], axis=1)
            pre = jnp.dot(xs[...], wu, preferred_element_type=F32)
            s = 1.0 / (1.0 + jnp.exp(-pre))
            hidden = (pre * s).astype(BF)
            hg = lax.dot_general(gs[...], wd, (((1,), (1,)), ((), ())), preferred_element_type=F32)
            pg = (hg * s * (1.0 + pre * (1.0 - s))).astype(BF)
            at = pl.ds(pl.multiple_of(j * BLK, BLK), BLK)
            hid[:, at] = hidden
            pgs[:, at] = pg
            dg = lax.dot_general(hidden, gs[...], (((0,), (0,)), ((), ())), preferred_element_type=F32)
            ug = lax.dot_general(pg, xs[...], (((0,), (0,)), ((), ())), preferred_element_type=F32)
            for k in range(8):
                GP[0, k, j] = ug[:, k * BLK:(k + 1) * BLK].astype(BF)
                GP[1, k, j] = dg[:, k * BLK:(k + 1) * BLK].astype(BF)

    def gp(m, a, o, q):
        return GP.at[m, fdev(a, zh if o else 1 - zh), pl.ds(q * JQ, JQ)]

    def rfa(m, s, o, q):
        return rf.at[m, s, o, pl.ds(q * JQ, JQ)]

    def f1(q):
        for o in (0, 1):
            h["r", 0, o, q] = send("g", gp(0, x2, o, q), rfa(0, 0, o, q), FP)
            h["r", 1, o, q] = send("g", gp(1, x2, o, q), rfa(1, 0, o, q), FM)
        for o in (0, 1):
            h["x", 0, o, q] = send("g", gp(0, xm, o, q), rfa(0, 1, o, q), FM)
            h["x", 1, o, q] = send("g", gp(1, xp, o, q), rfa(1, 1, o, q), FP)

    def add_tiles(dst, a, b, e=None):
        v = a[...].astype(F32) + b[...].astype(F32)
        if e is not None:
            v = v + e[...].astype(F32)
        dst[...] = v.astype(dst.dtype)

    def f2(q):
        for o in (0, 1):
            for m in (0, 1):
                arrive(h["r", m, o, q])
                part = gp(m, (xp, xm)[m], o, q)
                add_tiles(part, part, rfa(m, 0, o, q))
                h["s", m, o, q] = send("g", part, rfa(m, 2, o, q), (FP, FM)[m])

    def f3(q, o):
        for m in (0, 1):
            arrive(h["x", m, o, q])
            arrive(h["s", m, o, q])
            part = gp(m, x, o, q)
            z = zf.at[m, pl.ds(q * JQ, JQ)]
            if o == 0:
                add_tiles(part, part, rfa(m, 1, o, q), rfa(m, 2, o, q))
                h["zf", m, q] = send("g", part, z, FZ)
            else:
                out = (up_o, dn_o)[m].at[pl.ds(q * JQ, JQ)]
                add_tiles(out, part, rfa(m, 1, o, q), rfa(m, 2, o, q))

    def f4(q):
        for m in (0, 1):
            arrive(h["zf", m, q])
            out = (up_o, dn_o)[m].at[pl.ds(q * JQ, JQ)]
            add_tiles(out, out, zf.at[m, pl.ds(q * JQ, JQ)])

    def dense(m, first, last):
        @pl.loop(first, last)
        def _(i):
            if m == 0:
                w = jnp.concatenate([jnp.concatenate([WD[tab[j, 2 * i + b]] for b in (0, 1)], axis=1) for j in range(16)], axis=0)
                v = jnp.dot(hid[...], w, preferred_element_type=F32)
            else:
                w = jnp.concatenate([jnp.concatenate([WU[tab[16 + j, 2 * i + b]] for j in range(16)], axis=1) for b in (0, 1)], axis=0)
                v = lax.dot_general(pgs[...], w, (((1,), (1,)), ((), ())), preferred_element_type=F32)
            for b in (0, 1):
                A[m][2 * i + b] = v[:, b * BLK:(b + 1) * BLK].astype(BF)

    def chip(m, dy, o, core):
        return rows(A[m], tdev((y + dy) % 4, zl if o else 1 - zl, core))

    order = [(dy, o) for dy in (2, 3, 1, 0) for o in (0, 1)], [(dy, o) for dy in (2, 1, 3, 0) for o in (0, 1)]

    def t0(m):
        for dy, o in order[m]:
            h["c", m, dy, o] = send("g", chip(m, dy, o, 1 - c), ct.at[m, o * 4 + dy], TC)

    loads = {}

    def fetch(m, n):
        if n < 8:
            dy, o = order[m][n]
            loads[m, dy, o] = local(chip(m, dy, o, c), pt.at[m, n % 4]), n % 4

    def t_begin(m):
        t0(m)
        for n in range(4):
            fetch(m, n)

    def add_rows(dst, a, b, e=None):
        @pl.loop(0, 8)
        def _(i):
            q = pl.ds(i * 8, 8)
            v = a[q].astype(F32) + b[q].astype(F32)
            if e is not None:
                v = v + e[q].astype(F32)
            dst[q] = v.astype(dst.dtype)

    def pair(m, dy, o):
        arrive(h["c", m, dy, o])
        cp, slot = loads[m, dy, o]
        cp.wait()
        both = ct.at[m, o * 4 + dy]
        add_rows(both, both, pt.at[m, slot])
        fetch(m, order[m].index((dy, o)) + 4)
        return both

    def t1(m):
        for o in (0, 1):
            h["tr", m, o] = send("g", pair(m, 2, o), rt.at[m, 0, o], (TP, TM)[m])
        for o in (0, 1):
            h["tx", m, o] = send("g", pair(m, (3, 1)[m], o), rt.at[m, 1, o], (TM, TP)[m])

    def t2(m):
        for o in (0, 1):
            both = pair(m, (1, 3)[m], o)
            arrive(h["tr", m, o])
            add_rows(both, both, rt.at[m, 0, o])
            h["ts", m, o] = send("g", both, rt.at[m, 2, o], (TP, TM)[m])

    def t3(m, o):
        both = pair(m, 0, o)
        arrive(h["tx", m, o])
        arrive(h["ts", m, o])
        add_rows(both, both, rt.at[m, 1, o], rt.at[m, 2, o])
        if o == 0:
            h["tz", m] = send("g", both, zt.at[m], TZ)

    def t4(m):
        arrive(h["tz", m])
        for b in range(NB):
            v = ct[m, 4, b].astype(F32) + zt[m, b].astype(F32)
            (mix_o, inp_o)[m][:, b * BLK:(b + 1) * BLK] = v.astype(BF)

    products(0)
    f1(0)
    wn.rest(1)
    products(1)
    f1(1)
    wn.rest(2)
    products(2)
    f1(2)
    wn.rest(3)
    products(3)
    f1(3)
    for cp in sends["a"]:
        cp.wait_send()
    f2(0)
    dense(0, 0, 16)
    f2(1)
    dense(0, 16, 32)
    t_begin(0)
    dense(1, 0, 8)
    t1(0)
    f2(2)
    dense(1, 8, 32)
    t_begin(1)
    t2(0)
    f2(3)
    t1(1)
    f3(0, 0)
    f3(0, 1)
    t3(0, 0)
    f3(1, 0)
    f3(1, 1)
    t2(1)
    f4(0)
    t3(0, 1)
    f3(2, 0)
    f3(2, 1)
    f4(1)
    t4(0)
    f3(3, 0)
    t3(1, 0)
    f3(3, 1)
    t3(1, 1)
    f4(2)
    f4(3)
    t4(1)
    for cp in sends["w"] + sends["g"]:
        cp.wait_send()


def step(tok, og, upw, dnw, ui, di):
    sh = jax.ShapeDtypeStruct
    V = pltpu.VMEM
    T = (16, BLK, BLK)
    R = (NB, 24, BLK)
    hbm = pl.BlockSpec(memory_space=pl.ANY)
    vm = pl.BlockSpec(memory_space=pltpu.VMEM)
    nr = 14 * NQ + 14 * NH + 16 * NH + 14 * NQ + 30
    return pl.pallas_call(
        step_kernel,
        out_shape=(sh((24, D), BF), sh((24, D), BF), sh(T, F32), sh(T, F32)),
        in_specs=[hbm] * 4 + [vm] * 2,
        out_specs=(vm,) * 4,
        scratch_shapes=[V((2, 24, D), BF), V((2,) + R, BF), V((NB, 384, BLK), BF), V((NB, 384, BLK), BF), V((129, BLK, BLK), BF), V((129, BLK, BLK), BF),
                        V((384, 2048), BF), V((384, 2048), BF), V((384, 1024), BF), V((384, 1024), BF),
                        V((2, 8) + T, BF), V((2, 3, 2) + T, BF), V((2,) + T, BF),
                        V((2, 4) + R, BF), V((2, 8) + R, BF), V((2, 3, 2) + R, BF), V((2,) + R, BF),
                        V((32, BLK), jnp.int32), pltpu.SMEM((32, BLK), jnp.int32),
                        pltpu.SemaphoreType.DMA((nr,)), pltpu.SemaphoreType.DMA((nr,)), pltpu.SemaphoreType.DMA((24,))],
        compiler_params=pltpu.CompilerParams(collective_id=0, has_side_effects=True, vmem_limit_bytes=63 << 20),
        name="step",
    )(tok, og, upw, dnw, ui, di)


def body(tokens, out_grad, up_weight, down_weight, up_index, down_index):
    mixed, input_grad, up_grad, down_grad = step(tokens, out_grad, up_weight[:, 0], down_weight[:, 0], up_index, down_index)
    return mixed, input_grad, up_grad.transpose(0, 2, 1)[:, None], down_grad[:, None]


def solution(mesh):
    rows = P(("fsdp", "tensor"), None)
    tile = P("tensor", "fsdp", None, None)
    index = P("tensor", None)
    return jax.shard_map(
        body,
        mesh=mesh,
        in_specs=(rows, rows, tile, tile, index, index),
        out_specs=(rows, rows, tile, tile),
        check_vma=False,
    )
```
